768 devices in a mesh: tm: 24 (over z_lo, x), slab: 32 (over z_hi, y, core).
Axes of the slice: x: 4, y: 8, z: 12 (z_hi: 2, z_lo: 6; z = z_hi * 6 + z_lo), core: 2. Of those that a mesh axis runs over, the one named last changes fastest.
Arguments:
- initial: float32 [24, 16, 256, 16, 128], P('tm', None, 'slab'), may hold values from -6 to 6
- source: float32 [24, 256, 16, 128], P('tm', 'slab'), may hold values from -6 to 6
- decay_rate: float32 [256, 16, 128], P('slab'), may hold values from 0.01 to 0.2
- observed: float32 [24, 16, 256, 16, 128], P('tm', None, 'slab'), may hold values from -6 to 6
- release: int32 [24, 16], replicated, may hold values from 0 to 3
- smooth_taps: float32 [31], replicated, may hold values from 0.02 to 0.08
Outputs:
- source_gradient: float32 [24, 256, 2048], P('tm', None, 'slab')
- decay_gradient: float32 [24, 256, 2048], P('tm', None, 'slab')
The draws below stay inside these ranges and needn't reach their ends.
All inputs are finite; a program needn't handle non-finite values.
Results may differ from the reference program's by a relative error of at most 0.0003.
Values sent between devices are 32-bit elements; how exact they have to be, the bound alone decides.
No kernel may reach another device: no remote copies, remote signals or barrier semaphores. Data moves between devices by JAX's collectives and lax.ppermute only.
A program may use at most 32 MiB of HBM per device.

```python
import math
import jax
import jax.numpy as jnp
from jax import lax

CHANNELS = 16
STEPS = 4
TAPS = 31
NY = 16
NX = 128
NZ = 256
N_TM = 24


def set_ends(result, key, low, high):
    dims = result.shape
    place = [jax.random.randint(jax.random.fold_in(key, axis), (), 0, dims[axis]) for axis in range(len(dims))]
    result = result.at[tuple(place)].set(low)
    longest = dims.index(max(dims))
    place[longest] = (place[longest] + 1) % dims[longest]
    return result.at[tuple(place)].set(high)


def level_of(own_key, shape, pieces, low, top_value):
    def one(axis_at, blocks):
        draws = jax.random.uniform(jax.random.fold_in(jax.random.fold_in(own_key, 6), axis_at), (blocks,), jnp.float32, low / len(pieces), top_value / len(pieces))
        return jnp.repeat(jnp.exp(draws), shape[axis_at] // blocks).reshape((-1,) + (1,) * (len(shape) - axis_at - 1))

    gain = one(*pieces[0])
    for cut in pieces[1:]:
        gain = gain * one(*cut)
    return gain


def scatter_about(key, dims, width, reach, shards=(), kind=jnp.bfloat16):
    values = jax.random.normal(key, dims, jnp.float32) * width
    if len(shards) > 0:
        values = level_of(key, dims, shards, -0.22, 0.18) * values
    return jnp.clip(values, min=-reach, max=reach).astype(kind)


def setup_inputs(seed: int = 0) -> dict:
    keys = jax.random.split(jax.random.key(seed), 7)
    return {
        "initial": scatter_about(keys[0], (N_TM, CHANNELS, NZ, NY, NX), 1.0, 6.0, ((0, 24), (2, 32)), jnp.float32),
        "source": scatter_about(keys[1], (N_TM, NZ, NY, NX), 1.0, 6.0, ((0, 24), (1, 32)), jnp.float32),
        "decay_rate": jnp.clip(jnp.exp(math.log(0.2) - 2.9957323 * jax.random.uniform(keys[2], (NZ, NY, NX), jnp.float32) ** level_of(keys[2], (NZ, NY, NX), ((0, 32),), -0.2, 0.2)), 0.01, 0.2),
        "observed": scatter_about(keys[3], (N_TM, CHANNELS, NZ, NY, NX), 1.0, 6.0, ((0, 24), (2, 32)), jnp.float32),
        "release": set_ends(jax.random.randint(keys[4], (N_TM, CHANNELS), 0, STEPS), jax.random.fold_in(keys[4], 1), 0, STEPS - 1).astype(jnp.int32),
        "smooth_taps": jnp.clip(jax.random.uniform(keys[5], (TAPS,), jnp.float32, 0.02, 0.08), 0.02, 0.08),
    }


vertical_rate = 0.2
lateral_rate = 0.1


def apply_operator(current, decay_rate):
    padded = jnp.pad(current, ((0, 0), (1, 1), (1, 1), (1, 1)))
    vertical = padded[:, 2:, 1:-1, 1:-1] + padded[:, :-2, 1:-1, 1:-1]
    lateral = padded[:, 1:-1, 2:, 1:-1] + padded[:, 1:-1, :-2, 1:-1]
    lateral = lateral + padded[:, 1:-1, 1:-1, 2:] + padded[:, 1:-1, 1:-1, :-2]
    centre = 1.0 - 2.0 * vertical_rate - 4.0 * lateral_rate - decay_rate
    return current * centre + vertical_rate * vertical + lateral_rate * lateral


def smoothing_matrix(smooth_taps, depth):
    count = smooth_taps.shape[0]
    middle = (count - 1) // 2
    rows = jnp.arange(depth, dtype=jnp.int32)[:, None]
    columns = jnp.arange(depth, dtype=jnp.int32)[None, :]
    offset = columns - rows + middle
    match = (offset[:, :, None] == jnp.arange(count, dtype=jnp.int32)[None, None, :]).astype(smooth_taps.dtype)
    return jnp.sum(match * smooth_taps[None, None, :], axis=-1)


def reference(initial, source, decay_rate, observed, release, smooth_taps):
    depth = observed.shape[2]
    matrix = smoothing_matrix(smooth_taps, depth)
    rolled = jnp.roll(observed, N_TM // 2, axis=0)

    def window(items):
        start_field, release_field, target, release_row = items
        states = [start_field]
        current = start_field
        for step_index in range(STEPS):
            chosen = (release_row == step_index).astype(start_field.dtype)
            current = apply_operator(current, decay_rate) + chosen[:, None, None, None] * release_field[None]
            states.append(current)
        adjoint = states[STEPS] - target
        source_grad = jnp.zeros(release_field.shape, start_field.dtype)
        decay_grad = jnp.zeros(release_field.shape, start_field.dtype)
        for step_index in reversed(range(STEPS)):
            decay_grad = decay_grad - jnp.sum(adjoint * states[step_index], axis=0)
            chosen = (release_row == step_index).astype(start_field.dtype)
            source_grad = source_grad + jnp.sum(chosen[:, None, None, None] * adjoint, axis=0)
            if step_index > 0:
                adjoint = apply_operator(adjoint, decay_rate)
        both = jnp.stack([source_grad.reshape(depth, -1), decay_grad.reshape(depth, -1)])
        smoothed = jnp.einsum("ij,bjk->bik", matrix, both, precision=lax.Precision.HIGHEST)
        return smoothed[0], smoothed[1]

    source_rows, decay_rows = lax.map(window, (initial, source, rolled, release))
    return jnp.roll(source_rows, N_TM // 2, axis=0), jnp.roll(decay_rows, N_TM // 2, axis=0)
```

```python
import jax
import jax.numpy as jnp
from jax import lax
from jax.experimental import pallas as pl
from jax.experimental.pallas import tpu as pltpu
from jax.sharding import PartitionSpec as P

STEPS = 4
REACH = STEPS - 1
HALO = STEPS
CHUNKS = (10, 6)

vertical_rate = 0.2
lateral_rate = 0.1


def operator(value, centre):
    upper, lower = (half[1:-1] for half in value)
    row = lax.broadcasted_iota(jnp.int32, upper.shape, 1)
    lane = lax.broadcasted_iota(jnp.int32, upper.shape, 2)
    ny, nx = upper.shape[1:]
    upper_on, lower_on = pltpu.roll(upper, 1, 1), pltpu.roll(lower, 1, 1)
    upper_back, lower_back = pltpu.roll(upper, ny - 1, 1), pltpu.roll(lower, ny - 1, 1)
    sides = (
        jnp.where(row == 0, 0.0, upper_on) + jnp.where(row == ny - 1, lower_back, upper_back),
        jnp.where(row == 0, upper_on, lower_on) + jnp.where(row == ny - 1, 0.0, lower_back),
    )
    out = []
    for whole, middle, rate, side in zip(value, (upper, lower), centre, sides):
        left = jnp.where(lane == 0, 0.0, pltpu.roll(middle, 1, 2))
        right = jnp.where(lane == nx - 1, 0.0, pltpu.roll(middle, nx - 1, 2))
        vertical = whole[2:] + whole[:-2]
        out.append(middle * rate + vertical + (lateral_rate / vertical_rate) * (side + (left + right)))
    return tuple(out)


def inside(value, width, low, high):
    if width == 0:
        return value
    count = value.shape[0]
    return jnp.concatenate(
        [value[:width] * low, value[width : count - width], value[count - width :] * high], axis=0
    )


def padded(value):
    edge = jnp.zeros((2,) + value.shape[1:], value.dtype)
    return jnp.concatenate([edge, value, edge], axis=0)


def plus_middle(total, value):
    cut = (total.shape[0] - value.shape[0]) // 2
    return jnp.concatenate([total[:cut], total[cut:-cut] + value, total[-cut:]], axis=0)


def halves(value):
    cut = value.shape[1] // 2
    return value[:, :cut], value[:, cut:]


def one_channel(release, start, target, centre, field, low, high):
    scale = 1.0 / vertical_rate
    states = [start]
    for k in range(STEPS):
        part = slice(k, centre[0].shape[0] - k)
        value = operator(states[k], tuple(half[part] for half in centre))
        if release == k:
            value = tuple(v + scale ** (k + 1) * f[part] for v, f in zip(value, field))
        states.append(tuple(inside(v, REACH - k, low, high) for v in value))
    adjoint = tuple(s * scale**-STEPS - t for s, t in zip(states[STEPS], target))
    sums = None
    terms = []
    for k in reversed(range(STEPS)):
        if release == k:
            sums = tuple(a * scale ** (k - REACH) for a in adjoint)
        terms.append(tuple(a * s[1:-1] for a, s in zip(adjoint, states[k])))
        if k > 0:
            part = slice(k - 1, centre[0].shape[0] - (k - 1))
            adjoint = operator(
                tuple(padded(a) for a in adjoint), tuple(half[part] for half in centre)
            )
            adjoint = tuple(inside(a, STEPS - k, low, high) for a in adjoint)
    products = []
    for half in range(2):
        total = terms[-1][half]
        for term in reversed(terms[:-1]):
            total = plus_middle(total, term[half])
        products.append(total)
    return sums, products


def chunk_kernel(
    count,
    offset,
    first,
    last,
    scalars,
    middle,
    before,
    after,
    across,
    crossed,
    target,
    centre_in,
    field_in,
    *rest,
):
    if first:
        (*outs, sums, products, centre, field) = rest
    else:
        (sums_in, products_in, *outs, sums, products, centre, field) = rest
    c = pl.program_id(0)
    low = scalars[16].astype(jnp.float32)
    high = scalars[17].astype(jnp.float32)
    from_low = scalars[18].astype(jnp.float32)
    from_high = scalars[19].astype(jnp.float32)

    @pl.when(c == 0)
    def _():
        cut = HALO - REACH
        size = field.shape[0]
        field[...] = field_in[...]
        field[:REACH] += from_low * crossed[0, cut:]
        field[size - REACH :] += from_high * crossed[0, :REACH]
        centre[...] = centre_in[...]
        centre[:REACH] -= (from_low / vertical_rate) * crossed[1, cut:]
        centre[size - REACH :] -= (from_high / vertical_rate) * crossed[1, :REACH]
        if first:
            sums[...] = jnp.zeros_like(sums)
            products[...] = jnp.zeros_like(products)
        else:
            sums[...] = sums_in[...]
            products[...] = products_in[...]

    release = scalars[offset + c]
    rows = sums.shape[1] // 2

    def run(step):
        crossing = across[0]
        start = jnp.concatenate(
            [before[0] + from_low * crossing, middle[0], after[0] + from_high * crossing], axis=0
        )
        totals, found = one_channel(
            step, halves(start), halves(target[0, 0]), halves(centre[...]), halves(field[...]), low, high
        )
        for half, (total, product) in enumerate(zip(totals, found)):
            part = slice(half * rows, (half + 1) * rows)
            reach = slice(step, sums.shape[0] - step)
            sums[reach, part] += total
            products[:, part] -= product

    for k in range(STEPS):
        pl.when(release == k)(lambda k=k: run(k))

    @pl.when(c == count - 1)
    def _():
        if last:
            write_blocks(sums[...], products[...] * vertical_rate**REACH, outs[0])
        else:
            outs[0][...] = sums[...]
            outs[1][...] = products[...]


def write_blocks(first, second, out):
    edge = jnp.zeros((1,) + first.shape[1:], first.dtype)
    first = jnp.concatenate([edge, first, edge], axis=0)
    second = jnp.concatenate([edge, second, edge], axis=0)
    half = first.shape[-1] // 2
    lane = lax.broadcasted_iota(jnp.int32, first.shape, 2)
    even = jnp.where(lane < half, first, pltpu.roll(second, half, 2))
    odd = jnp.where(lane < half, pltpu.roll(first, half, 2), second)
    out[:, 0] = jnp.transpose(even, (1, 0, 2))
    out[:, 1] = jnp.transpose(odd, (1, 0, 2))


def vmem():
    return pl.BlockSpec(memory_space=pltpu.VMEM)


def run_chunk(count, offset, last, scalars, middle, before, after, across, observed, centre, field, carried):
    layers, ny, nx = middle.shape[1:]
    first = not carried
    wide = (layers + 2 * REACH, ny, nx)
    flat = pl.BlockSpec(wide, lambda c: (0, 0, 0))
    if last:
        shapes = (jax.ShapeDtypeStruct((ny, 2, layers + 2 * HALO, nx), jnp.float32),)
        out_specs = (pl.BlockSpec(shapes[0].shape, lambda c: (0, 0, 0, 0)),)
    else:
        shapes = (jax.ShapeDtypeStruct(wide, jnp.float32),) * 2
        out_specs = (flat, flat)

    def kernel(*refs):
        chunk_kernel(count, offset, first, last, *refs)

    return pl.pallas_call(
        kernel,
        grid=(count,),
        out_shape=shapes,
        in_specs=[
            pl.BlockSpec(memory_space=pltpu.SMEM),
            pl.BlockSpec((1, layers, ny, nx), lambda c: (c, 0, 0, 0)),
            pl.BlockSpec((1, HALO, ny, nx), lambda c: (c, before.shape[1] // HALO - 1, 0, 0)),
            pl.BlockSpec((1, HALO, ny, nx), lambda c: (c, 0, 0, 0)),
            pl.BlockSpec((1, HALO, ny, nx), lambda c: (offset + c + 2, 0, 0, 0)),
            pl.BlockSpec((2, HALO, ny, nx), lambda c: (0, 0, 0, 0)),
            pl.BlockSpec((1, 1, layers, ny, nx), lambda c: (0, offset + c, 0, 0, 0)),
            flat,
            flat,
        ]
        + [flat] * len(carried),
        out_specs=out_specs,
        scratch_shapes=[pltpu.VMEM(wide, jnp.float32)] * 4,
        cost_estimate=pl.CostEstimate(
            flops=count * 4000000, bytes_accessed=count * 250000, transcendentals=0
        ),
        name="last_chunk" if last else "chunk",
    )(scalars, middle, before, after, across, across, observed, centre, field, *carried)


def prepare_kernel(taps, source, decay, before, after, centre, field, matrix):
    def spread(mid, slot):
        layers = mid.shape[0]
        return jnp.concatenate(
            [before[slot, layers - REACH :], mid, after[slot, :REACH]], axis=0
        )

    field[...] = spread(source[0], 0)
    rate = 1.0 - 2.0 * vertical_rate - 4.0 * lateral_rate - spread(decay[...], 1)
    centre[...] = rate * (1.0 / vertical_rate)

    depth = matrix.shape[1]
    layers = source.shape[1]
    block = layers + 2 * HALO
    count = taps.shape[0]

    def fill(slab, _):
        shape = (block, depth)
        layer = lax.broadcasted_iota(jnp.int32, shape, 0) + (slab * layers - HALO)
        offset = layer - lax.broadcasted_iota(jnp.int32, shape, 1) + (count - 1) // 2
        offset = jnp.where((layer >= 0) & (layer < depth), offset, -1)
        value = jnp.zeros(shape, jnp.float32)
        for tap in range(count):
            value = jnp.where(offset == tap, taps[tap], value)
        matrix[pl.ds(pl.multiple_of(slab * block, block), block), :] = value
        return 0

    lax.fori_loop(0, matrix.shape[0] // block, fill, 0)


def prepare(slabs, taps, source, decay, before, after):
    layers, ny, nx = decay.shape
    wide = jax.ShapeDtypeStruct((layers + 2 * REACH, ny, nx), jnp.float32)
    matrix = jax.ShapeDtypeStruct((slabs * (layers + 2 * HALO), slabs * layers), jnp.float32)
    smem = pl.BlockSpec(memory_space=pltpu.SMEM)
    return pl.pallas_call(
        prepare_kernel,
        grid=(1,),
        out_shape=(wide, wide, matrix),
        in_specs=[smem]
        + [pl.BlockSpec(a.shape, lambda c, n=a.ndim: (0,) * n) for a in (source, decay, before, after)],
        out_specs=tuple(pl.BlockSpec(a.shape, lambda c, n=len(a.shape): (0,) * n) for a in (wide, wide, matrix)),
        cost_estimate=pl.CostEstimate(flops=8000000, bytes_accessed=2000000, transcendentals=0),
        name="prepare",
    )(taps, source, decay, before, after)


def smooth_kernel(matrix, columns, source_out, decay_out):
    result = lax.dot_general(
        columns[...],
        matrix[...],
        (((0,), (0,)), ((), ())),
        preferred_element_type=jnp.float32,
        precision=lax.Precision.HIGHEST,
    )
    half = result.shape[0] // 2
    source_out[...] = result[:half]
    decay_out[...] = result[half:]


def smooth(matrix, columns):
    depth = matrix.shape[1]
    half = columns.shape[1] // 2
    shape = jax.ShapeDtypeStruct((half, depth), jnp.float32)
    return pl.pallas_call(
        smooth_kernel,
        out_shape=(shape, shape),
        in_specs=[vmem(), vmem()],
        out_specs=(vmem(), vmem()),
        name="smooth",
    )(matrix, columns)


def body(initial, source, decay_rate, observed, release, smooth_taps):
    groups = lax.axis_size("tm")
    slabs = lax.axis_size("slab")
    half_way = groups // 2
    centre_cut = slabs // 2
    tm_index = lax.axis_index("tm")
    slab_index = lax.axis_index("slab")
    own_initial = initial[0]
    layers = own_initial.shape[1]

    across_tm = [(i, (i + half_way) % groups) for i in range(groups)]
    upward = [(s, s + 1) for s in range(slabs - 1) if s != centre_cut - 1]
    downward = [(t, s) for s, t in upward]
    crossing_pairs = []
    for i, j in across_tm:
        crossing_pairs.append((i * slabs + centre_cut - 1, j * slabs + centre_cut))
        crossing_pairs.append((i * slabs + centre_cut, j * slabs + centre_cut - 1))

    arrived_source = lax.ppermute(source, "tm", across_tm)
    arrived = []
    offset = 0
    for count in CHUNKS:
        arrived.append(lax.ppermute(own_initial[offset : offset + count], "tm", across_tm))
        offset += count

    def edge_of(stack):
        return jnp.where(slab_index == centre_cut, stack[:, :HALO], stack[:, layers - HALO :])

    edge = jnp.concatenate([edge_of(a) for a in (source, decay_rate[None], own_initial)], axis=0)
    across = lax.ppermute(edge, ("tm", "slab"), crossing_pairs)

    partner = (tm_index + half_way) % groups
    flags = jnp.stack(
        [
            slab_index > 0,
            slab_index < slabs - 1,
            slab_index == centre_cut,
            slab_index == centre_cut - 1,
        ]
    ).astype(jnp.int32)
    row = lax.dynamic_index_in_dim(release, partner, 0, keepdims=False)
    scalars = jnp.concatenate([row, flags])

    both = jnp.concatenate([arrived_source, decay_rate[None]], axis=0)
    before = lax.ppermute(both, "slab", upward)
    after = lax.ppermute(both, "slab", downward)
    centre, field, matrix = prepare(
        slabs, smooth_taps, arrived_source, decay_rate, before, after
    )

    carried = ()
    offset = 0
    for index, count in enumerate(CHUNKS):
        middle = arrived[index]
        last = index == len(CHUNKS) - 1
        before = lax.ppermute(middle[:, layers - HALO :] if last else middle, "slab", upward)
        after = lax.ppermute(middle[:, :HALO] if last else middle, "slab", downward)
        carried = run_chunk(
            count,
            offset,
            last,
            scalars,
            middle,
            before,
            after,
            across,
            observed,
            centre,
            field,
            carried,
        )
        offset += count

    width = layers + 2 * HALO
    blocks = carried[0].reshape(slabs, width, carried[0].shape[-1])
    columns = lax.all_to_all(blocks, "slab", split_axis=0, concat_axis=0, tiled=True)
    columns = columns.reshape(slabs * width, blocks.shape[-1])
    smoothed = smooth(matrix, columns)
    return (smoothed[0].T[None], smoothed[1].T[None])


def solution(mesh):
    placed = (
        P("tm", None, "slab", None, None),
        P("tm", "slab", None, None),
        P("slab", None, None),
        P("tm", None, "slab", None, None),
        P(),
        P(),
    )

    return jax.shard_map(
        body,
        mesh=mesh,
        in_specs=placed,
        out_specs=(P("tm", None, "slab"), P("tm", None, "slab")),
        check_vma=False,
    )
```

```python
import jax
import jax.numpy as jnp
from jax import lax
from jax.experimental import pallas as pl
from jax.experimental.pallas import tpu as pltpu
from jax.sharding import PartitionSpec as P

STEPS = 4
REACH = STEPS - 1
HALO = STEPS
CHUNKS = (11, 5)

vertical_rate = 0.2
lateral_rate = 0.1


def operator(value, centre):
    upper, lower = (half[1:-1] for half in value)
    row = lax.broadcasted_iota(jnp.int32, upper.shape, 1)
    lane = lax.broadcasted_iota(jnp.int32, upper.shape, 2)
    ny, nx = upper.shape[1:]
    upper_on, lower_on = pltpu.roll(upper, 1, 1), pltpu.roll(lower, 1, 1)
    upper_back, lower_back = pltpu.roll(upper, ny - 1, 1), pltpu.roll(lower, ny - 1, 1)
    sides = (
        jnp.where(row == 0, 0.0, upper_on) + jnp.where(row == ny - 1, lower_back, upper_back),
        jnp.where(row == 0, upper_on, lower_on) + jnp.where(row == ny - 1, 0.0, lower_back),
    )
    out = []
    for whole, middle, rate, side in zip(value, (upper, lower), centre, sides):
        left = jnp.where(lane == 0, 0.0, pltpu.roll(middle, 1, 2))
        right = jnp.where(lane == nx - 1, 0.0, pltpu.roll(middle, nx - 1, 2))
        vertical = whole[2:] + whole[:-2]
        out.append(middle * rate + vertical + (lateral_rate / vertical_rate) * (side + (left + right)))
    return tuple(out)


def inside(value, width, low, high):
    if width == 0:
        return value
    count = value.shape[0]
    return jnp.concatenate(
        [value[:width] * low, value[width : count - width], value[count - width :] * high], axis=0
    )


def padded(value):
    edge = jnp.zeros((2,) + value.shape[1:], value.dtype)
    return jnp.concatenate([edge, value, edge], axis=0)


def plus_middle(total, value):
    cut = (total.shape[0] - value.shape[0]) // 2
    return jnp.concatenate([total[:cut], total[cut:-cut] + value, total[-cut:]], axis=0)


def halves(value):
    cut = value.shape[1] // 2
    return value[:, :cut], value[:, cut:]


def one_channel(release, start, target, centre, field, low, high):
    scale = 1.0 / vertical_rate
    states = [start]
    for k in range(STEPS):
        part = slice(k, centre[0].shape[0] - k)
        value = operator(states[k], tuple(half[part] for half in centre))
        if release == k:
            value = tuple(v + scale ** (k + 1) * f[part] for v, f in zip(value, field))
        states.append(tuple(inside(v, REACH - k, low, high) for v in value))
    adjoint = tuple(s * scale**-STEPS - t for s, t in zip(states[STEPS], target))
    sums = None
    terms = []
    for k in reversed(range(STEPS)):
        if release == k:
            sums = tuple(a * scale ** (k - REACH) for a in adjoint)
        terms.append(tuple(a * s[1:-1] for a, s in zip(adjoint, states[k])))
        if k > 0:
            part = slice(k - 1, centre[0].shape[0] - (k - 1))
            adjoint = operator(
                tuple(padded(a) for a in adjoint), tuple(half[part] for half in centre)
            )
            adjoint = tuple(inside(a, STEPS - k, low, high) for a in adjoint)
    products = []
    for half in range(2):
        total = terms[-1][half]
        for term in reversed(terms[:-1]):
            total = plus_middle(total, term[half])
        products.append(total)
    return sums, products


def chunk_kernel(
    count,
    offset,
    first,
    last,
    scalars,
    middle,
    before,
    after,
    across,
    crossed,
    target,
    centre_in,
    field_in,
    *rest,
):
    if first:
        (*outs, sums, products, centre, field) = rest
    else:
        (sums_in, products_in, *outs, sums, products, centre, field) = rest
    c = pl.program_id(0)
    low = scalars[16].astype(jnp.float32)
    high = scalars[17].astype(jnp.float32)
    from_low = scalars[18].astype(jnp.float32)
    from_high = scalars[19].astype(jnp.float32)

    @pl.when(c == 0)
    def _():
        cut = HALO - REACH
        size = field.shape[0]
        field[...] = field_in[...]
        field[:REACH] += from_low * crossed[0, cut:]
        field[size - REACH :] += from_high * crossed[0, :REACH]
        centre[...] = centre_in[...]
        centre[:REACH] -= (from_low / vertical_rate) * crossed[1, cut:]
        centre[size - REACH :] -= (from_high / vertical_rate) * crossed[1, :REACH]
        if first:
            sums[...] = jnp.zeros_like(sums)
            products[...] = jnp.zeros_like(products)
        else:
            sums[...] = sums_in[...]
            products[...] = products_in[...]

    release = scalars[offset + c]
    rows = sums.shape[1] // 2

    def run(step):
        crossing = across[0]
        start = jnp.concatenate(
            [before[0] + from_low * crossing, middle[0], after[0] + from_high * crossing], axis=0
        )
        totals, found = one_channel(
            step, halves(start), halves(target[0, 0]), halves(centre[...]), halves(field[...]), low, high
        )
        for half, (total, product) in enumerate(zip(totals, found)):
            part = slice(half * rows, (half + 1) * rows)
            reach = slice(step, sums.shape[0] - step)
            sums[reach, part] += total
            products[:, part] -= product

    for k in range(STEPS):
        pl.when(release == k)(lambda k=k: run(k))

    @pl.when(c == count - 1)
    def _():
        if last:
            write_blocks(sums[...], products[...] * vertical_rate**REACH, outs[0])
        else:
            outs[0][...] = sums[...]
            outs[1][...] = products[...]


def write_blocks(first, second, out):
    edge = jnp.zeros((1,) + first.shape[1:], first.dtype)
    first = jnp.concatenate([edge, first, edge], axis=0)
    second = jnp.concatenate([edge, second, edge], axis=0)
    half = first.shape[-1] // 2
    lane = lax.broadcasted_iota(jnp.int32, first.shape, 2)
    even = jnp.where(lane < half, first, pltpu.roll(second, half, 2))
    odd = jnp.where(lane < half, pltpu.roll(first, half, 2), second)
    out[:, 0] = jnp.transpose(even, (1, 0, 2))
    out[:, 1] = jnp.transpose(odd, (1, 0, 2))


def vmem():
    return pl.BlockSpec(memory_space=pltpu.VMEM)


def run_chunk(count, offset, last, scalars, middle, before, after, across, observed, centre, field, carried):
    layers, ny, nx = middle.shape[1:]
    first = not carried
    wide = (layers + 2 * REACH, ny, nx)
    flat = pl.BlockSpec(wide, lambda c: (0, 0, 0))
    if last:
        shapes = (jax.ShapeDtypeStruct((ny, 2, layers + 2 * HALO, nx), jnp.float32),)
        out_specs = (pl.BlockSpec(shapes[0].shape, lambda c: (0, 0, 0, 0)),)
    else:
        shapes = (jax.ShapeDtypeStruct(wide, jnp.float32),) * 2
        out_specs = (flat, flat)

    def kernel(*refs):
        chunk_kernel(count, offset, first, last, *refs)

    return pl.pallas_call(
        kernel,
        grid=(count,),
        out_shape=shapes,
        in_specs=[
            pl.BlockSpec(memory_space=pltpu.SMEM),
            pl.BlockSpec((1, layers, ny, nx), lambda c: (c, 0, 0, 0)),
            pl.BlockSpec((1, HALO, ny, nx), lambda c: (c, before.shape[1] // HALO - 1, 0, 0)),
            pl.BlockSpec((1, HALO, ny, nx), lambda c: (c, 0, 0, 0)),
            pl.BlockSpec((1, HALO, ny, nx), lambda c: (offset + c + 2, 0, 0, 0)),
            pl.BlockSpec((2, HALO, ny, nx), lambda c: (0, 0, 0, 0)),
            pl.BlockSpec((1, 1, layers, ny, nx), lambda c: (0, offset + c, 0, 0, 0)),
            flat,
            flat,
        ]
        + [flat] * len(carried),
        out_specs=out_specs,
        scratch_shapes=[pltpu.VMEM(wide, jnp.float32)] * 4,
        cost_estimate=pl.CostEstimate(
            flops=count * 4000000, bytes_accessed=count * 250000, transcendentals=0
        ),
        compiler_params=pltpu.CompilerParams(vmem_limit_bytes=16 << 20),
        name="last_chunk" if last else "chunk",
    )(scalars, middle, before, after, across, across, observed, centre, field, *carried)


def prepare_kernel(taps, source, decay, before, after, centre, field, matrix):
    def spread(mid, slot):
        layers = mid.shape[0]
        return jnp.concatenate(
            [before[slot, layers - REACH :], mid, after[slot, :REACH]], axis=0
        )

    field[...] = spread(source[0], 0)
    rate = 1.0 - 2.0 * vertical_rate - 4.0 * lateral_rate - spread(decay[...], 1)
    centre[...] = rate * (1.0 / vertical_rate)

    depth = matrix.shape[1]
    layers = source.shape[1]
    block = layers + 2 * HALO
    count = taps.shape[0]

    def fill(slab, _):
        shape = (block, depth)
        layer = lax.broadcasted_iota(jnp.int32, shape, 0) + (slab * layers - HALO)
        offset = layer - lax.broadcasted_iota(jnp.int32, shape, 1) + (count - 1) // 2
        offset = jnp.where((layer >= 0) & (layer < depth), offset, -1)
        value = jnp.zeros(shape, jnp.float32)
        for tap in range(count):
            value = jnp.where(offset == tap, taps[tap], value)
        matrix[pl.ds(pl.multiple_of(slab * block, block), block), :] = value
        return 0

    lax.fori_loop(0, matrix.shape[0] // block, fill, 0)


def prepare(slabs, taps, source, decay, before, after):
    layers, ny, nx = decay.shape
    wide = jax.ShapeDtypeStruct((layers + 2 * REACH, ny, nx), jnp.float32)
    matrix = jax.ShapeDtypeStruct((slabs * (layers + 2 * HALO), slabs * layers), jnp.float32)
    smem = pl.BlockSpec(memory_space=pltpu.SMEM)
    return pl.pallas_call(
        prepare_kernel,
        grid=(1,),
        out_shape=(wide, wide, matrix),
        in_specs=[smem]
        + [pl.BlockSpec(a.shape, lambda c, n=a.ndim: (0,) * n) for a in (source, decay, before, after)],
        out_specs=tuple(pl.BlockSpec(a.shape, lambda c, n=len(a.shape): (0,) * n) for a in (wide, wide, matrix)),
        cost_estimate=pl.CostEstimate(flops=8000000, bytes_accessed=2000000, transcendentals=0),
        compiler_params=pltpu.CompilerParams(vmem_limit_bytes=8 << 20),
        name="prepare",
    )(taps, source, decay, before, after)


def smooth_kernel(matrix, columns, source_out, decay_out):
    result = lax.dot_general(
        columns[...],
        matrix[...],
        (((0,), (0,)), ((), ())),
        preferred_element_type=jnp.float32,
        precision=lax.Precision.HIGHEST,
    )
    half = result.shape[0] // 2
    source_out[...] = result[:half]
    decay_out[...] = result[half:]


def smooth(matrix, columns):
    depth = matrix.shape[1]
    half = columns.shape[1] // 2
    shape = jax.ShapeDtypeStruct((half, depth), jnp.float32)
    return pl.pallas_call(
        smooth_kernel,
        out_shape=(shape, shape),
        in_specs=[vmem(), vmem()],
        out_specs=(vmem(), vmem()),
        compiler_params=pltpu.CompilerParams(vmem_limit_bytes=8 << 20),
        name="smooth",
    )(matrix, columns)


def body(initial, source, decay_rate, observed, release, smooth_taps):
    groups = lax.axis_size("tm")
    slabs = lax.axis_size("slab")
    half_way = groups // 2
    centre_cut = slabs // 2
    tm_index = lax.axis_index("tm")
    slab_index = lax.axis_index("slab")
    own_initial = initial[0]
    layers = own_initial.shape[1]

    across_tm = [(i, (i + half_way) % groups) for i in range(groups)]
    upward = [(s, s + 1) for s in range(slabs - 1) if s != centre_cut - 1]
    downward = [(t, s) for s, t in upward]
    crossing_pairs = []
    for i, j in across_tm:
        crossing_pairs.append((i * slabs + centre_cut - 1, j * slabs + centre_cut))
        crossing_pairs.append((i * slabs + centre_cut, j * slabs + centre_cut - 1))

    arrived_source = lax.ppermute(source, "tm", across_tm)
    arrived = []
    offset = 0
    for count in CHUNKS:
        arrived.append(lax.ppermute(own_initial[offset : offset + count], "tm", across_tm))
        offset += count

    def edge_of(stack):
        return jnp.where(slab_index == centre_cut, stack[:, :HALO], stack[:, layers - HALO :])

    edge = jnp.concatenate([edge_of(a) for a in (source, decay_rate[None], own_initial)], axis=0)
    across = lax.ppermute(edge, ("tm", "slab"), crossing_pairs)

    partner = (tm_index + half_way) % groups
    flags = jnp.stack(
        [
            slab_index > 0,
            slab_index < slabs - 1,
            slab_index == centre_cut,
            slab_index == centre_cut - 1,
        ]
    ).astype(jnp.int32)
    row = lax.dynamic_index_in_dim(release, partner, 0, keepdims=False)
    scalars = jnp.concatenate([row, flags])

    both = jnp.concatenate([arrived_source, decay_rate[None]], axis=0)
    before = lax.ppermute(both, "slab", upward)
    after = lax.ppermute(both, "slab", downward)
    centre, field, matrix = prepare(
        slabs, smooth_taps, arrived_source, decay_rate, before, after
    )

    carried = ()
    offset = 0
    for index, count in enumerate(CHUNKS):
        middle = arrived[index]
        last = index == len(CHUNKS) - 1
        before = lax.ppermute(middle[:, layers - HALO :] if last else middle, "slab", upward)
        after = lax.ppermute(middle[:, :HALO] if last else middle, "slab", downward)
        carried = run_chunk(
            count,
            offset,
            last,
            scalars,
            middle,
            before,
            after,
            across,
            observed,
            centre,
            field,
            carried,
        )
        offset += count

    width = layers + 2 * HALO
    blocks = carried[0].reshape(slabs, width, carried[0].shape[-1])
    columns = lax.all_to_all(blocks, "slab", split_axis=0, concat_axis=0, tiled=True)
    columns = columns.reshape(slabs * width, blocks.shape[-1])
    smoothed = smooth(matrix, columns)
    return (smoothed[0].T[None], smoothed[1].T[None])


def solution(mesh):
    placed = (
        P("tm", None, "slab", None, None),
        P("tm", "slab", None, None),
        P("slab", None, None),
        P("tm", None, "slab", None, None),
        P(),
        P(),
    )

    return jax.shard_map(
        body,
        mesh=mesh,
        in_specs=placed,
        out_specs=(P("tm", None, "slab"), P("tm", None, "slab")),
        check_vma=False,
    )
```
